512 devices in a mesh: lat: 16 (over z_hi, y, core), lon: 32 (over x, z_lo).
Axes of the slice: x: 4, y: 4, z: 16 (z_hi: 2, z_lo: 8; z = z_hi * 8 + z_lo), core: 2. Of those that a mesh axis runs over, the one named last changes fastest.
Arguments:
- bands: bfloat16 [16, 256, 320, 512], P('lat', 'lon'), may hold values from -6 to 6
- avail: int32 [16, 256, 10], P('lat', 'lon'), may hold values from 0 to 1, as said below
- latent_query: bfloat16 [4, 512], replicated, may hold values from -3 to 3
- w_band: bfloat16 [512, 1024], replicated, may hold values from -3.0935922 to 3.0935922
- w_mix: bfloat16 [512, 1536], replicated, may hold values from -3 to 3
- w_out: bfloat16 [512, 512], replicated, may hold values from -0.19921875 to 0.19921875
- offsets: int32 [5, 2], replicated, may hold values from -1 to 1, as said below
Outputs:
- encoded: bfloat16 [16, 256, 4, 512], P('lat', 'lon')
The draws below stay inside these ranges and needn't reach their ends.
Inputs may be any that keep to these rules, and one draw needn't show every extreme that they name: `avail`: each patch has at least one available block. `offsets`: row 0 is (0, 0), rows 1 and 2 are (0, -1) and (0, 1), row 3 has latitude offset -1 and row 4 latitude offset +1; all rows differ.
All inputs are finite; a program needn't handle non-finite values.
Results may differ from the reference program's by a relative error of at most 0.03.
The reference program's roundings to bfloat16 on the way count: a program that leaves them out, or rounds other values in their place, can miss the bound.
Values may be sent and summed in bfloat16 or wider, within the bound.
No kernel may reach another device: no remote copies, remote signals or barrier semaphores. Data moves between devices by JAX's collectives and lax.ppermute only.
A program may use at most 64 MiB of HBM per device.

```python
import jax
import jax.numpy as jnp
from jax import lax

D = 512
HEADS = 16
HEAD = 32
BANDS = 320
BLOCK = 32
LATENTS = 4
NOFF = 5
NBLK = 10
LAT_ROWS = 16
LON_COLS = 256


def draw_bands(key, part):
    whole_shape = (LAT_ROWS, LON_COLS, BANDS, D)
    patch_shape = (LAT_ROWS, LON_COLS, 1, D)
    noise = jnp.clip(jax.random.normal(jax.random.fold_in(key, 11), whole_shape, jnp.float32), -4.0, 4.0)
    shared = 1.5 * jnp.clip(jax.random.normal(jax.random.fold_in(key, 12), patch_shape, jnp.float32), -4.0, 4.0)
    return jnp.clip(noise + shared, -6.0, 6.0).astype(jnp.bfloat16)


def draw_avail(key, part):
    shape_all = (LAT_ROWS, LON_COLS, NBLK)
    row_iota = lax.broadcasted_iota(jnp.int32, shape_all, 0)
    threshold = 15 + 80 * row_iota // max(LAT_ROWS - 1, 1)
    dice_roll = jax.random.randint(jax.random.fold_in(key, 1), shape_all, 0, 100)
    open_draw = (dice_roll < threshold).astype(jnp.int32)
    chosen = jax.random.randint(jax.random.fold_in(key, 2), (LAT_ROWS, LON_COLS, 1), 0, NBLK)
    forced = (lax.broadcasted_iota(jnp.int32, shape_all, 2) == chosen).astype(jnp.int32)
    return jnp.maximum(open_draw, forced)


def draw_latent_query(key, part):
    entries = 0.3 * jnp.clip(jax.random.normal(jax.random.fold_in(key, 3), (LATENTS, D), jnp.float32), -6.0, 6.0)
    return entries.astype(jnp.bfloat16)


def draw_w_band(key, part):
    fan_scale = D ** (-0.5)
    entries = jnp.clip(jax.random.normal(jax.random.fold_in(key, 13), (D, 2 * D), jnp.float32), -6.0, 6.0) * fan_scale
    return entries.astype(jnp.bfloat16)


def draw_w_mix(key, part):
    entries = jnp.clip(jax.random.normal(jax.random.fold_in(key, 5), (D, 3 * D), jnp.float32), -6.0, 6.0) * D ** (-0.5)
    return entries.astype(jnp.bfloat16)


def draw_offsets(key, part):
    lon_reach = jax.random.randint(jax.random.fold_in(key, 7), (2,), -1, 2).astype(jnp.int32)
    lat_column = jnp.array([0, 0, 0, -1, 1], jnp.int32)
    fixed_lon = jnp.array([0, -1, 1, 0, 0], jnp.int32)
    picker = jnp.array([0, 0, 0, 1, 1], jnp.int32)
    second = jnp.array([0, 0, 0, 1, 0], jnp.int32)
    lon_column = fixed_lon + picker * (second * lon_reach[0] + (1 - second) * lon_reach[1])
    return jnp.stack([lat_column, lon_column], axis=1)


def setup_inputs(seed: int = 0) -> dict:
    arg_keys = jax.random.split(jax.random.key(seed), 8)
    bands = draw_bands(jax.random.fold_in(arg_keys[7], 71), 0)
    avail = draw_avail(jax.random.fold_in(arg_keys[7], 71), 0)
    latent_query = draw_latent_query(jax.random.fold_in(arg_keys[7], 71), 0)
    w_band = draw_w_band(jax.random.fold_in(arg_keys[7], 71), 0)
    w_mix = draw_w_mix(jax.random.fold_in(arg_keys[7], 71), 0)
    w_out = jnp.clip(jax.random.uniform(arg_keys[5], (D, D), jnp.float32, -0.19921875, 0.19921875), -0.19921875, 0.19921875).astype(jnp.bfloat16)
    offsets = draw_offsets(jax.random.fold_in(arg_keys[7], 71), 0)
    return {"bands": bands, "avail": avail, "latent_query": latent_query, "w_band": w_band, "w_mix": w_mix, "w_out": w_out, "offsets": offsets}


EPS = 1e-06
NEG = -1e+30

def rms_rows(values):
    values = values.astype(jnp.float32)
    return values * lax.rsqrt(lax.optimization_barrier(jnp.mean(values * values, axis=-1, keepdims=True)) + EPS)

def softmax_weights(scores):
    peak_value = lax.optimization_barrier(jnp.max(scores, axis=-1, keepdims=True))
    exponent = jnp.exp(scores - peak_value)
    return (exponent / lax.optimization_barrier(jnp.sum(exponent, axis=-1, keepdims=True))).astype(jnp.bfloat16)

def pool_row(row_bands, row_avail, latent_query, w_band):
    columns = row_bands.shape[0]
    score_scale = HEAD ** (-0.5)
    normed = rms_rows(row_bands).astype(jnp.bfloat16)
    key_value = jnp.dot(normed.reshape(-1, D), w_band, preferred_element_type=jnp.float32).astype(jnp.bfloat16)
    key_value = key_value.reshape(columns, BANDS, 2, HEADS, HEAD).astype(jnp.float32)
    queries = latent_query.reshape(LATENTS, HEADS, HEAD).astype(jnp.float32)
    scores = jnp.einsum('lhe,pbhe->plhb', queries, key_value[:, :, 0]) * score_scale
    open_band = jnp.repeat(row_avail, BLOCK, axis=-1) > 0
    scores = jnp.where(open_band[:, None, None, :], scores, NEG)
    weights = softmax_weights(scores).astype(jnp.float32)
    pooled = jnp.einsum('plhb,pbhe->plhe', weights, key_value[:, :, 1])
    latent = pooled.reshape(columns, LATENTS, D) + latent_query.astype(jnp.float32)
    return rms_rows(latent)

def reference(bands, avail, latent_query, w_band, w_mix, w_out, offsets):
    lat_rows = bands.shape[0]
    columns = bands.shape[1]
    groups = HEADS // 2
    half_width = D // 2
    score_scale = HEAD ** (-0.5)
    normal = lax.map(lambda row_item: pool_row(row_item[0], row_item[1], latent_query, w_band), (bands, avail))
    mixture = jnp.dot(normal.astype(jnp.bfloat16).reshape(-1, D), w_mix, preferred_element_type=jnp.float32).astype(jnp.bfloat16)
    mixture = mixture.reshape(lat_rows, columns, LATENTS, 3 * D)
    queries = mixture[..., :D].astype(jnp.float32).reshape(lat_rows, columns, LATENTS, HEADS, HEAD)
    near_pairs = mixture[..., D:2 * D]
    zonal_pairs = mixture[..., 2 * D:]
    framed = jnp.pad(near_pairs, ((1, 1), (0, 0), (0, 0), (0, 0)))
    row_index = jnp.arange(lat_rows, dtype=jnp.int32)
    near_keys = []
    near_open = []
    for offset_slot in range(NOFF):
        step_lat = offsets[offset_slot, 0]
        step_lon = offsets[offset_slot, 1]
        shifted = lax.dynamic_slice_in_dim(framed, (1 + step_lat).astype(jnp.int32), lat_rows, 0)
        shifted = jnp.roll(shifted, -step_lon, axis=1)
        near_keys.append(shifted)
        target = row_index + step_lat
        near_open.append((target >= 0) & (target < lat_rows))
    near_keys = jnp.stack(near_keys, axis=2).reshape(lat_rows, columns, NOFF * LATENTS, 2, groups, HEAD).astype(jnp.float32)
    open_keys = jnp.repeat(jnp.stack(near_open, axis=1), LATENTS, axis=1)
    scores = jnp.einsum('ijqhe,ijkhe->ijhqk', queries[..., :groups, :], near_keys[..., 0, :, :]) * score_scale
    scores = jnp.where(open_keys[:, None, None, None, :], scores, NEG)
    weights = softmax_weights(scores).astype(jnp.float32)
    near_out = jnp.einsum('ijhqk,ijkhe->ijqhe', weights, near_keys[..., 1, :, :])
    row_keys = zonal_pairs.reshape(lat_rows, columns * LATENTS, 2, groups, HEAD).astype(jnp.float32)
    scores = jnp.einsum('ijqhe,ikhe->ijhqk', queries[..., groups:, :], row_keys[:, :, 0]) * score_scale
    weights = softmax_weights(scores).astype(jnp.float32)
    zonal_out = jnp.einsum('ijhqk,ikhe->ijqhe', weights, row_keys[:, :, 1])
    attended = jnp.concatenate([near_out.reshape(lat_rows, columns, LATENTS, half_width), zonal_out.reshape(lat_rows, columns, LATENTS, half_width)], axis=-1).astype(jnp.bfloat16)
    update = jnp.dot(attended.reshape(-1, D), w_out, preferred_element_type=jnp.float32).reshape(lat_rows, columns, LATENTS, D)
    return (normal + update).astype(jnp.bfloat16)
```

```python
import jax
import jax.numpy as jnp
from jax import lax
from jax.experimental import pallas as pl
from jax.experimental.pallas import tpu as pltpu
from jax.sharding import Mesh, PartitionSpec as P

D = 512
HEADS = 16
HEAD = 32
BANDS = 320
BLOCK = 32
LATENTS = 4
NBLK = 10
HALF = D // 2
GROUPS = HEADS // 2
COLS = 8
TOK = COLS * LATENTS
LON = 32
LAT = 16
SCALE = HEAD ** (-0.5)

EPS = 1e-06
NEG = -1e30

LON_AXES = ("x", "q", "m", "p")
CLASS_AXES = ("x", "m")

F32 = jnp.float32
BF16 = jnp.bfloat16
CONTRACT_LAST = (((1,), (1,)), ((), ()))


def iota(shape, dim):
    return lax.broadcasted_iota(jnp.int32, shape, dim)


def rms(values):
    return values * lax.rsqrt(jnp.mean(values * values, axis=-1, keepdims=True) + EPS)


def softmax_weights(scores):
    exponent = jnp.exp(scores - jnp.max(scores, axis=-1, keepdims=True))
    return (exponent / jnp.sum(exponent, axis=-1, keepdims=True)).astype(BF16)


def lon_index():
    return lax.axis_index("x") * 8 + lax.axis_index("q") * 4 + lax.axis_index("m") * 2 + lax.axis_index("p")


PER_STEP = 2


def pool_kernel(
    avail_ref, bands_ref, query_ref, w_band_ref, w_mix_hbm, send_ref, normal_ref, near_ref, nearq_ref,
    qbd_ref, latent_ref, w_mix_ref, halo_ref, sem,
):
    step = pl.program_id(0)
    w_mix_copy = pltpu.make_async_copy(w_mix_hbm, w_mix_ref, sem)
    query = query_ref[...].astype(F32)

    @pl.when(step == 0)
    def _():
        w_mix_copy.start()
        own_head = iota((HEADS, D), 1) // HEAD == iota((HEADS, D), 0)
        for l in range(LATENTS):
            row = jnp.broadcast_to(query[l : l + 1], (HEADS, D))
            qbd_ref[l * HEADS : (l + 1) * HEADS, :] = jnp.where(own_head, row, 0.0).astype(BF16)

    own_lane = iota((HEADS, D), 1) // HEAD == iota((HEADS, D), 0)
    band_block = iota((1, BANDS), 1) // BLOCK
    tokens = bands_ref[0].reshape(PER_STEP * BANDS, D).astype(F32)
    normed = rms(tokens).astype(BF16)
    key_value = jnp.dot(normed, w_band_ref[...], preferred_element_type=F32).astype(BF16)
    for i in range(PER_STEP):
        patch = step * PER_STEP + i
        rows = slice(i * BANDS, (i + 1) * BANDS)
        scores = (
            lax.dot_general(qbd_ref[...], key_value[rows, :D], CONTRACT_LAST, preferred_element_type=F32)
            * SCALE
        )
        is_open = jnp.zeros((1, BANDS), jnp.int32)
        for b in range(NBLK):
            is_open = jnp.where(band_block == b, avail_ref[0, patch, b], is_open)
        scores = jnp.where(is_open > 0, scores, NEG)
        weights = softmax_weights(scores)
        pooled = jnp.dot(weights, key_value[rows, D:], preferred_element_type=F32)
        for l in range(LATENTS):
            part = jnp.where(own_lane, pooled[l * HEADS : (l + 1) * HEADS], 0.0)
            latent_ref[step, i * LATENTS + l : i * LATENTS + l + 1, :] = (
                jnp.sum(part, axis=0, keepdims=True) + query[l : l + 1]
            )

    @pl.when(step == COLS // PER_STEP - 1)
    def _():
        w_mix_copy.wait()
        normal = rms(latent_ref[...].reshape(TOK, D))
        normal_ref[...] = normal
        mixture = jnp.dot(normal.astype(BF16), w_mix_ref[...], preferred_element_type=F32)
        near_ref[...] = mixture[:, D : 2 * D].astype(BF16)
        nearq_ref[...] = mixture[:, :HALF].astype(BF16)
        for side, first in ((0, 0), (1, TOK - LATENTS)):
            for j in range(4):
                halo_ref[side, j * LATENTS : (j + 1) * LATENTS, :] = mixture[
                    first : first + LATENTS, D + j * 128 : D + (j + 1) * 128
                ]
        to_west = halo_ref[0].astype(BF16)
        to_east = halo_ref[1].astype(BF16)
        me = lon_index()
        east = lax.rem(me + 1, LON)
        west = lax.rem(me + LON - 1, LON)
        half = TOK // 2
        zeros = jnp.zeros((half, HEAD), F32)
        for g in range(GROUPS):
            q = mixture[:, HALF + g * HEAD : HALF + (g + 1) * HEAD]
            k = mixture[:, 2 * D + g * HEAD : 2 * D + (g + 1) * HEAD]
            v = mixture[:, 2 * D + HALF + g * HEAD : 2 * D + HALF + (g + 1) * HEAD]
            pairs = jnp.concatenate([k[:half], v[:half], k[half:], v[half:]], axis=1).astype(BF16)
            slot = jnp.concatenate([q[:half], zeros, q[half:], zeros], axis=1).astype(BF16)
            for c in range(4):
                dest = (g // 2) * 8 + (c // 2) * 4 + (g % 2) * 2 + c % 2
                send_ref[dest, :half, :] = pairs
                send_ref[dest, half:, :] = jnp.where(dest == east, to_east, jnp.where(dest == west, to_west, slot))


def pool(bands, avail, latent_query, w_band, w_mix):
    whole = lambda *shape: pl.BlockSpec(shape, lambda i: (0,) * len(shape))
    return pl.pallas_call(
        pool_kernel,
        grid=(COLS // PER_STEP,),
        in_specs=[
            pl.BlockSpec(memory_space=pltpu.SMEM),
            pl.BlockSpec((1, PER_STEP, BANDS, D), lambda i: (0, i, 0, 0)),
            whole(LATENTS, D),
            whole(D, 2 * D),
            pl.BlockSpec(memory_space=pl.ANY),
        ],
        out_specs=[whole(LON, TOK, 128), whole(TOK, D), whole(TOK, D), whole(TOK, HALF)],
        out_shape=[
            jax.ShapeDtypeStruct((LON, TOK, 128), BF16),
            jax.ShapeDtypeStruct((TOK, D), F32),
            jax.ShapeDtypeStruct((TOK, D), BF16),
            jax.ShapeDtypeStruct((TOK, HALF), BF16),
        ],
        scratch_shapes=[
            pltpu.VMEM((LATENTS * HEADS, D), BF16),
            pltpu.VMEM((COLS // PER_STEP, PER_STEP * LATENTS, D), F32),
            pltpu.VMEM((D, 3 * D), BF16),
            pltpu.VMEM((2, 16, 128), F32),
            pltpu.SemaphoreType.DMA,
        ],
        name="pool",
    )(avail, bands, latent_query, w_band, w_mix)


def window_kernel(offsets_ref, near_ref, got_ref, own_ref, up_ref, down_ref, ext_ref):
    me = lon_index()
    half = TOK // 2
    west = got_ref[lax.rem(me + LON - 1, LON), half:, :].astype(F32)
    east = got_ref[lax.rem(me + 1, LON), half:, :].astype(F32)
    for j in range(4):
        lanes = slice(j * 128, (j + 1) * 128)
        ext_ref[:LATENTS, lanes] = west[j * LATENTS : (j + 1) * LATENTS]
        ext_ref[LATENTS + TOK :, lanes] = east[j * LATENTS : (j + 1) * LATENTS]
    ext_ref[LATENTS : LATENTS + TOK, :] = near_ref[...].astype(F32)
    shifted = [ext_ref[i * LATENTS : i * LATENTS + TOK, :].astype(BF16) for i in range(3)]
    own_ref[:TOK] = shifted[1]
    own_ref[TOK : 2 * TOK] = shifted[0]
    own_ref[2 * TOK :] = shifted[2]
    for ref, slot in ((down_ref, 3), (up_ref, 4)):
        step = offsets_ref[slot, 1]
        ref[...] = jnp.where(step == 0, shifted[1], jnp.where(step < 0, shifted[0], shifted[2]))


def windows(offsets, near, got):
    return pl.pallas_call(
        window_kernel,
        in_specs=[
            pl.BlockSpec(memory_space=pltpu.SMEM),
            pl.BlockSpec(memory_space=pltpu.VMEM),
            pl.BlockSpec(memory_space=pltpu.VMEM),
        ],
        out_shape=[
            jax.ShapeDtypeStruct((3 * TOK, D), BF16),
            jax.ShapeDtypeStruct((TOK, D), BF16),
            jax.ShapeDtypeStruct((TOK, D), BF16),
        ],
        scratch_shapes=[pltpu.VMEM((TOK + 2 * LATENTS, D), F32)],
        name="windows",
    )(offsets, near, got)


def zonal_kernel(got_ref, out_ref):
    half = TOK // 2
    qp = lax.axis_index("q") * 4 + lax.axis_index("p")
    pairs = got_ref[:, :half, :].reshape(LON * half, 128)
    slots = jnp.concatenate([got_ref[(c // 2) * 8 + (c % 2) * 2 + qp, half:, :] for c in range(8)], axis=0)
    slots = slots.astype(F32)
    lane = iota((8 * half, 128), 1)
    first = jnp.where(lane < HEAD, slots, 0.0)
    second = jnp.where((lane >= 64) & (lane < 64 + HEAD), slots, 0.0)
    low = jnp.concatenate([first, pltpu.roll(second, 64, 1)], axis=0).astype(BF16)
    high = jnp.concatenate([pltpu.roll(first, 64, 1), second], axis=0).astype(BF16)
    scores_low = lax.dot_general(low, pairs, CONTRACT_LAST, preferred_element_type=F32) * SCALE
    scores_high = lax.dot_general(high, pairs, CONTRACT_LAST, preferred_element_type=F32) * SCALE
    peak = jnp.maximum(
        jnp.max(scores_low, axis=-1, keepdims=True), jnp.max(scores_high, axis=-1, keepdims=True)
    )
    exp_low = jnp.exp(scores_low - peak)
    exp_high = jnp.exp(scores_high - peak)
    total = jnp.sum(exp_low, axis=-1, keepdims=True) + jnp.sum(exp_high, axis=-1, keepdims=True)
    weights_low = (exp_low / total).astype(BF16)
    weights_high = (exp_high / total).astype(BF16)
    out_low = jnp.dot(weights_low, pairs, preferred_element_type=F32)
    out_high = jnp.dot(weights_high, pairs, preferred_element_type=F32)
    rows = 8 * half
    for_first = out_low[:rows] + pltpu.roll(out_high[:rows], 64, 1)
    for_second = pltpu.roll(out_low[rows:], 64, 1) + out_high[rows:]
    out_ref[...] = jnp.where(lane < 64, for_first, for_second).astype(BF16).reshape(8, half, 128)


def zonal(got):
    return pl.pallas_call(
        zonal_kernel,
        out_shape=jax.ShapeDtypeStruct((GROUPS, TOK // 2, 128), BF16),
        name="zonal",
    )(got)


def final_kernel(own_ref, north_ref, south_ref, nearq_ref, back_ref, normal_ref, w_out_ref, out_ref, zonal_ref):
    keys = jnp.concatenate([own_ref[...], north_ref[...], south_ref[...]], axis=0)
    count = 5 * TOK
    query = nearq_ref[...]
    head_lane = iota((TOK, HALF), 1) // HEAD
    spread = jnp.concatenate(
        [jnp.where(head_lane == h, query, jnp.zeros_like(query)) for h in range(GROUPS)], axis=0
    )
    scores = lax.dot_general(spread, keys[:, :HALF], CONTRACT_LAST, preferred_element_type=F32) * SCALE
    row = iota((GROUPS * TOK, count), 0)
    col = iota((GROUPS * TOK, count), 1)
    lat = lax.axis_index("lat")
    from_lat = jnp.where(col < 3 * TOK, lat, jnp.where(col < 4 * TOK, lat - 1, lat + 1))
    same = (row % TOK) // LATENTS == (col % TOK) // LATENTS
    scores = jnp.where(same & (from_lat >= 0) & (from_lat < LAT), scores, NEG)
    weights = softmax_weights(scores)
    spread_out = jnp.dot(weights, keys[:, HALF:], preferred_element_type=F32)
    near_out = jnp.zeros((TOK, HALF), F32)
    for h in range(GROUPS):
        near_out += jnp.where(head_lane == h, spread_out[h * TOK : (h + 1) * TOK], 0.0)

    half = TOK // 2
    lane_head = iota((half, 128), 1) // HEAD
    for part in range(2):
        for tile in range(2):
            block = jnp.zeros((half, 128), F32)
            for i in range(4):
                piece = back_ref[tile * 4 + i].astype(F32)
                shift = (i * HEAD - HEAD - part * 64) % 128
                if shift:
                    piece = pltpu.roll(piece, shift, 1)
                block = jnp.where(lane_head == i, piece, block)
            zonal_ref[part * half : (part + 1) * half, tile * 128 : (tile + 1) * 128] = block.astype(BF16)
    attended = jnp.concatenate([near_out.astype(BF16), zonal_ref[...]], axis=1)
    update = jnp.dot(attended, w_out_ref[...], preferred_element_type=F32)
    encoded = (normal_ref[...] + update).astype(BF16)
    for c in range(COLS):
        out_ref[0, c] = encoded[c * LATENTS : (c + 1) * LATENTS]


def final(own, north, south, nearq, back, normal, w_out):
    return pl.pallas_call(
        final_kernel,
        out_shape=jax.ShapeDtypeStruct((1, COLS, LATENTS, D), BF16),
        scratch_shapes=[pltpu.VMEM((TOK, HALF), BF16)],
        name="final",
    )(own, north, south, nearq, back, normal, w_out)


def per_device(bands, avail, latent_query, w_band, w_mix, w_out, offsets):
    send, normal, near, nearq = pool(bands, avail, latent_query, w_band, w_mix)
    got = lax.all_to_all(send, LON_AXES, 0, 0, tiled=True)
    own, up, down = windows(offsets, near, got)
    north = lax.ppermute(down, "lat", [(i, i + 1) for i in range(LAT - 1)])
    south = lax.ppermute(up, "lat", [(i + 1, i) for i in range(LAT - 1)])
    back = lax.all_to_all(zonal(got), CLASS_AXES, 0, 0, tiled=True)
    return final(own, north, south, nearq, back, normal, w_out)


def solution(mesh):
    grid = Mesh(mesh.devices.reshape(LAT, 4, 2, 2, 2), ("lat",) + LON_AXES)
    patches = P("lat", LON_AXES, None, None)
    return jax.shard_map(
        per_device,
        mesh=grid,
        in_specs=(patches, P("lat", LON_AXES, None), P(), P(), P(), P(), P()),
        out_specs=patches,
        check_vma=False,
    )
```

```python
import jax
import jax.numpy as jnp
from jax import lax
from jax.experimental import pallas as pl
from jax.experimental.pallas import tpu as pltpu
from jax.sharding import Mesh, PartitionSpec as P


D = 512
HEADS = 16
HEAD = 32
BANDS = 320
BLOCK = 32
LATENTS = 4
NBLK = 10
HALF = D // 2
GROUPS = HEADS // 2
COLS = 8
TOK = COLS * LATENTS
LON = 32
LAT = 16
SCALE = HEAD ** (-0.5)

EPS = 1e-06
NEG = -1e30

LON_AXES = ("x", "q", "m", "p")
CLASS_AXES = ("x", "m")

F32 = jnp.float32
BF16 = jnp.bfloat16
CONTRACT_LAST = (((1,), (1,)), ((), ()))


def iota(shape, dim):
    return lax.broadcasted_iota(jnp.int32, shape, dim)


def rms(values):
    return values * lax.rsqrt(jnp.mean(values * values, axis=-1, keepdims=True) + EPS)


def softmax_weights(scores):
    exponent = jnp.exp(scores - jnp.max(scores, axis=-1, keepdims=True))
    return (exponent / jnp.sum(exponent, axis=-1, keepdims=True)).astype(BF16)


def lon_index():
    return lax.axis_index("x") * 8 + lax.axis_index("q") * 4 + lax.axis_index("m") * 2 + lax.axis_index("p")


PER_STEP = 2


def pool_kernel(
    avail_ref, bands_ref, query_ref, w_band_ref, w_mix_hbm, send_ref, normal_ref, near_ref, nearq_ref,
    qbd_ref, latent_ref, w_mix_ref, halo_ref, sem,
):
    step = pl.program_id(0)
    w_mix_copy = pltpu.make_async_copy(w_mix_hbm, w_mix_ref, sem)
    query = query_ref[...].astype(F32)

    @pl.when(step == 0)
    def _():
        w_mix_copy.start()
        own_head = iota((HEADS, D), 1) // HEAD == iota((HEADS, D), 0)
        for l in range(LATENTS):
            row = jnp.broadcast_to(query[l : l + 1], (HEADS, D))
            qbd_ref[l * HEADS : (l + 1) * HEADS, :] = jnp.where(own_head, row, 0.0).astype(BF16)

    own_lane = iota((HEADS, D), 1) // HEAD == iota((HEADS, D), 0)
    band_block = iota((1, BANDS), 1) // BLOCK
    tokens = bands_ref[0].reshape(PER_STEP * BANDS, D).astype(F32)
    normed = rms(tokens).astype(BF16)
    key_value = jnp.dot(normed, w_band_ref[...], preferred_element_type=F32).astype(BF16)
    for i in range(PER_STEP):
        patch = step * PER_STEP + i
        rows = slice(i * BANDS, (i + 1) * BANDS)
        scores = (
            lax.dot_general(qbd_ref[...], key_value[rows, :D], CONTRACT_LAST, preferred_element_type=F32)
            * SCALE
        )
        is_open = jnp.zeros((1, BANDS), jnp.int32)
        for b in range(NBLK):
            is_open = jnp.where(band_block == b, avail_ref[0, patch, b], is_open)
        scores = jnp.where(is_open > 0, scores, NEG)
        weights = softmax_weights(scores)
        pooled = jnp.dot(weights, key_value[rows, D:], preferred_element_type=F32)
        for l in range(LATENTS):
            part = jnp.where(own_lane, pooled[l * HEADS : (l + 1) * HEADS], 0.0)
            latent_ref[step, i * LATENTS + l : i * LATENTS + l + 1, :] = (
                jnp.sum(part, axis=0, keepdims=True) + query[l : l + 1]
            )

    @pl.when(step == COLS // PER_STEP - 1)
    def _():
        w_mix_copy.wait()
        normal = rms(latent_ref[...].reshape(TOK, D))
        normal_ref[...] = normal
        mixture = jnp.dot(normal.astype(BF16), w_mix_ref[...], preferred_element_type=F32)
        near_ref[...] = mixture[:, D : 2 * D].astype(BF16)
        nearq_ref[...] = mixture[:, :HALF].astype(BF16)
        for side, first in ((0, 0), (1, TOK - LATENTS)):
            for j in range(4):
                halo_ref[side, j * LATENTS : (j + 1) * LATENTS, :] = mixture[
                    first : first + LATENTS, D + j * 128 : D + (j + 1) * 128
                ]
        to_west = halo_ref[0].astype(BF16)
        to_east = halo_ref[1].astype(BF16)
        me = lon_index()
        east = lax.rem(me + 1, LON)
        west = lax.rem(me + LON - 1, LON)
        half = TOK // 2
        zeros = jnp.zeros((half, HEAD), F32)
        for g in range(GROUPS):
            q = mixture[:, HALF + g * HEAD : HALF + (g + 1) * HEAD]
            k = mixture[:, 2 * D + g * HEAD : 2 * D + (g + 1) * HEAD]
            v = mixture[:, 2 * D + HALF + g * HEAD : 2 * D + HALF + (g + 1) * HEAD]
            pairs = jnp.concatenate([k[:half], v[:half], k[half:], v[half:]], axis=1).astype(BF16)
            slot = jnp.concatenate([q[:half], zeros, q[half:], zeros], axis=1).astype(BF16)
            for c in range(4):
                dest = (g // 2) * 8 + (c // 2) * 4 + (g % 2) * 2 + c % 2
                send_ref[dest, :half, :] = pairs
                send_ref[dest, half:, :] = jnp.where(dest == east, to_east, jnp.where(dest == west, to_west, slot))


def pool(bands, avail, latent_query, w_band, w_mix):
    whole = lambda *shape: pl.BlockSpec(shape, lambda i: (0,) * len(shape))
    return pl.pallas_call(
        pool_kernel,
        grid=(COLS // PER_STEP,),
        in_specs=[
            pl.BlockSpec(memory_space=pltpu.SMEM),
            pl.BlockSpec((1, PER_STEP, BANDS, D), lambda i: (0, i, 0, 0)),
            whole(LATENTS, D),
            whole(D, 2 * D),
            pl.BlockSpec(memory_space=pl.ANY),
        ],
        out_specs=[whole(LON, TOK, 128), whole(TOK, D), whole(TOK, D), whole(TOK, HALF)],
        out_shape=[
            jax.ShapeDtypeStruct((LON, TOK, 128), BF16),
            jax.ShapeDtypeStruct((TOK, D), F32),
            jax.ShapeDtypeStruct((TOK, D), BF16),
            jax.ShapeDtypeStruct((TOK, HALF), BF16),
        ],
        scratch_shapes=[
            pltpu.VMEM((LATENTS * HEADS, D), BF16),
            pltpu.VMEM((COLS // PER_STEP, PER_STEP * LATENTS, D), F32),
            pltpu.VMEM((D, 3 * D), BF16),
            pltpu.VMEM((2, 16, 128), F32),
            pltpu.SemaphoreType.DMA,
        ],
        name="pool",
    )(avail, bands, latent_query, w_band, w_mix)


def window_kernel(offsets_ref, near_ref, got_ref, own_ref, chip_ref, far_ref, ext_ref):
    me = lon_index()
    half = TOK // 2
    west = got_ref[lax.rem(me + LON - 1, LON), half:, :].astype(F32)
    east = got_ref[lax.rem(me + 1, LON), half:, :].astype(F32)
    for j in range(4):
        lanes = slice(j * 128, (j + 1) * 128)
        ext_ref[:LATENTS, lanes] = west[j * LATENTS : (j + 1) * LATENTS]
        ext_ref[LATENTS + TOK :, lanes] = east[j * LATENTS : (j + 1) * LATENTS]
    ext_ref[LATENTS : LATENTS + TOK, :] = near_ref[...].astype(F32)
    shifted = [ext_ref[i * LATENTS : i * LATENTS + TOK, :].astype(BF16) for i in range(3)]
    own_ref[:TOK] = shifted[1]
    own_ref[TOK : 2 * TOK] = shifted[0]
    own_ref[2 * TOK :] = shifted[2]
    is_even = lax.rem(lax.axis_index("lat"), 2) == 0
    south_step = offsets_ref[1, 3]
    north_step = offsets_ref[1, 4]
    for ref, step in (
        (chip_ref, jnp.where(is_even, south_step, north_step)),
        (far_ref, jnp.where(is_even, north_step, south_step)),
    ):
        ref[...] = jnp.where(step == 0, shifted[1], jnp.where(step < 0, shifted[0], shifted[2]))


def windows(offsets, near, got):
    return pl.pallas_call(
        window_kernel,
        in_specs=[
            pl.BlockSpec(memory_space=pltpu.SMEM),
            pl.BlockSpec(memory_space=pltpu.VMEM),
            pl.BlockSpec(memory_space=pltpu.VMEM),
        ],
        out_shape=[
            jax.ShapeDtypeStruct((3 * TOK, D), BF16),
            jax.ShapeDtypeStruct((TOK, D), BF16),
            jax.ShapeDtypeStruct((TOK, D), BF16),
        ],
        scratch_shapes=[pltpu.VMEM((TOK + 2 * LATENTS, D), F32)],
        name="windows",
    )(offsets, near, got)


def zonal_kernel(got_ref, out_ref):
    half = TOK // 2
    qp = lax.axis_index("q") * 4 + lax.axis_index("p")
    pairs = got_ref[:, :half, :].reshape(LON * half, 128)
    slots = jnp.concatenate([got_ref[(c // 2) * 8 + (c % 2) * 2 + qp, half:, :] for c in range(8)], axis=0)
    slots = slots.astype(F32)
    lane = iota((8 * half, 128), 1)
    first = jnp.where(lane < HEAD, slots, 0.0)
    second = jnp.where((lane >= 64) & (lane < 64 + HEAD), slots, 0.0)
    low = jnp.concatenate([first, pltpu.roll(second, 64, 1)], axis=0).astype(BF16)
    high = jnp.concatenate([pltpu.roll(first, 64, 1), second], axis=0).astype(BF16)
    scores_low = lax.dot_general(low, pairs, CONTRACT_LAST, preferred_element_type=F32) * SCALE
    scores_high = lax.dot_general(high, pairs, CONTRACT_LAST, preferred_element_type=F32) * SCALE
    peak = jnp.maximum(
        jnp.max(scores_low, axis=-1, keepdims=True), jnp.max(scores_high, axis=-1, keepdims=True)
    )
    exp_low = jnp.exp(scores_low - peak)
    exp_high = jnp.exp(scores_high - peak)
    total = jnp.sum(exp_low, axis=-1, keepdims=True) + jnp.sum(exp_high, axis=-1, keepdims=True)
    weights_low = (exp_low / total).astype(BF16)
    weights_high = (exp_high / total).astype(BF16)
    out_low = jnp.dot(weights_low, pairs, preferred_element_type=F32)
    out_high = jnp.dot(weights_high, pairs, preferred_element_type=F32)
    rows = 8 * half
    for_first = out_low[:rows] + pltpu.roll(out_high[:rows], 64, 1)
    for_second = pltpu.roll(out_low[rows:], 64, 1) + out_high[rows:]
    out_ref[...] = jnp.where(lane < 64, for_first, for_second).astype(BF16).reshape(8, half, 128)


def zonal(got):
    return pl.pallas_call(
        zonal_kernel,
        out_shape=jax.ShapeDtypeStruct((GROUPS, TOK // 2, 128), BF16),
        name="zonal",
    )(got)


def final_kernel(own_ref, chip_ref, far_ref, nearq_ref, back_ref, normal_ref, w_out_ref, out_ref, zonal_ref):
    keys = jnp.concatenate([own_ref[...], chip_ref[...], far_ref[...]], axis=0)
    count = 5 * TOK
    query = nearq_ref[...]
    head_lane = iota((TOK, HALF), 1) // HEAD
    spread = jnp.concatenate(
        [jnp.where(head_lane == h, query, jnp.zeros_like(query)) for h in range(GROUPS)], axis=0
    )
    scores = lax.dot_general(spread, keys[:, :HALF], CONTRACT_LAST, preferred_element_type=F32) * SCALE
    row = iota((GROUPS * TOK, count), 0)
    col = iota((GROUPS * TOK, count), 1)
    lat = lax.axis_index("lat")
    inside = jnp.where((lat > 0) & (lat < LAT - 1), count, 4 * TOK)
    same = (row % TOK) // LATENTS == (col % TOK) // LATENTS
    scores = jnp.where(same & (col < inside), scores, NEG)
    weights = softmax_weights(scores)
    spread_out = jnp.dot(weights, keys[:, HALF:], preferred_element_type=F32)
    near_out = jnp.zeros((TOK, HALF), F32)
    for h in range(GROUPS):
        near_out += jnp.where(head_lane == h, spread_out[h * TOK : (h + 1) * TOK], 0.0)

    half = TOK // 2
    lane_head = iota((half, 128), 1) // HEAD
    for part in range(2):
        for tile in range(2):
            block = jnp.zeros((half, 128), F32)
            for i in range(4):
                piece = back_ref[tile * 4 + i].astype(F32)
                shift = (i * HEAD - HEAD - part * 64) % 128
                if shift:
                    piece = pltpu.roll(piece, shift, 1)
                block = jnp.where(lane_head == i, piece, block)
            zonal_ref[part * half : (part + 1) * half, tile * 128 : (tile + 1) * 128] = block.astype(BF16)
    attended = jnp.concatenate([near_out.astype(BF16), zonal_ref[...]], axis=1)
    update = jnp.dot(attended, w_out_ref[...], preferred_element_type=F32)
    encoded = (normal_ref[...] + update).astype(BF16)
    for c in range(COLS):
        out_ref[0, c] = encoded[c * LATENTS : (c + 1) * LATENTS]


def final(own, chip, far, nearq, back, normal, w_out):
    return pl.pallas_call(
        final_kernel,
        out_shape=jax.ShapeDtypeStruct((1, COLS, LATENTS, D), BF16),
        scratch_shapes=[pltpu.VMEM((TOK, HALF), BF16)],
        name="final",
    )(own, chip, far, nearq, back, normal, w_out)


def per_device(bands, avail, latent_query, w_band, w_mix, w_out, offsets):
    send, normal, near, nearq = pool(bands, avail, latent_query, w_band, w_mix)
    got = lax.all_to_all(send, LON_AXES, 0, 0, tiled=True)
    own, to_chip, to_far = windows(offsets.T, near, got)
    far = lax.ppermute(to_far, "lat", [(i, i + 1 if i % 2 else i - 1) for i in range(1, LAT - 1)])
    chip = lax.ppermute(to_chip, "lat", [(i, i ^ 1) for i in range(LAT)])
    mine = zonal(got)
    back = lax.all_to_all(mine, CLASS_AXES, 0, 0, tiled=True)
    return final(own, chip, far, nearq, back, normal, w_out)


def solution(mesh):
    grid = Mesh(mesh.devices.reshape(LAT, 4, 2, 2, 2), ("lat",) + LON_AXES)
    patches = P("lat", LON_AXES, None, None)
    return jax.shard_map(
        per_device,
        mesh=grid,
        in_specs=(patches, P("lat", LON_AXES, None), P(), P(), P(), P(), P()),
        out_specs=patches,
        check_vma=False,
    )
```
